32 devices in a mesh: stream: 4 (over x, core), tm: 8 (over z, y).
Axes of the slice: x: 2, y: 2, z: 4, core: 2. Of those that a mesh axis runs over, the one named last changes fastest.
Arguments:
- frames_in: bfloat16 [8, 3072, 1024], P('stream', 'tm'), may hold values from -45 to 45
- w_qkv: bfloat16 [1024, 3072], replicated, may hold values from -1 to 1
- grad_out: bfloat16 [8, 3072, 1024], P('stream', 'tm'), may hold values from -6 to 6
Outputs:
- grad_in: bfloat16 [8, 3072, 1024], P('stream', 'tm')
- grad_w: float32 [1024, 3072], P(('stream', 'tm'))
The draws below stay inside these ranges and needn't reach their ends.
All inputs are finite; a program needn't handle non-finite values.
Results may differ from the reference program's by a relative error of at most 0.015.
Values may be sent and summed in bfloat16 or wider, within the bound.
A program may use at most 192 MiB of HBM per device.

```python
import jax
import jax.numpy as jnp
from jax import lax

D = 1024
HEADS = 8
F_DEV = 384
RECORDINGS = 8
FRAMES = 3072


def draw_frames_in(key, part):
    keys = jax.random.split(key, 1)
    base = jax.random.truncated_normal(keys[0], -4.0, 4.0, (RECORDINGS, FRAMES, D), jnp.float32)
    return base.astype(jnp.bfloat16)


def draw_w_qkv(key, part):
    keys = jax.random.split(key, 1)
    weights = jax.random.truncated_normal(keys[0], -5.0, 5.0, (D, 3 * D), jnp.float32) * D ** (-0.5)
    return weights.astype(jnp.bfloat16)


def shard_levels(rng, shape, pieces, least, largest):
    def one(dim, parts):
        heights = jax.random.uniform(jax.random.fold_in(jax.random.fold_in(rng, 6), dim), (parts,), jnp.float32, least / len(pieces), largest / len(pieces))
        return jnp.repeat(jnp.exp(heights), shape[dim] // parts).reshape((-1,) + (1,) * (len(shape) - dim - 1))

    factor_of = one(*pieces[0])
    for cut in pieces[1:]:
        factor_of = factor_of * one(*cut)
    return factor_of


def normal_values(rng, shape, spread, limit, cuts=(), held_as=jnp.bfloat16):
    entries = spread * jax.random.normal(rng, shape, jnp.float32)
    if cuts:
        entries = entries * shard_levels(rng, shape, cuts, -0.22, 0.18)
    return jnp.clip(entries, -limit, limit).astype(held_as)


def setup_inputs(seed: int = 0) -> dict:
    arg_keys = jax.random.split(jax.random.key(seed), 4)
    return {
        "frames_in": draw_frames_in(jax.random.fold_in(arg_keys[3], 71), 0),
        "w_qkv": draw_w_qkv(jax.random.fold_in(arg_keys[3], 71), 0),
        "grad_out": normal_values(arg_keys[2], (RECORDINGS, FRAMES, D), 1.0, 6.0, ((0, 4), (1, 8))),
    }


def reference(frames_in, w_qkv, grad_out):
    records, frame_count, model_width = frames_in.shape
    head_size = model_width // HEADS
    blocks = frame_count // F_DEV
    score_scale = head_size ** -0.5
    hp = lax.Precision.HIGHEST

    def one_record(pair):
        frames_one, grad_one = pair
        qkv = jnp.dot(frames_one, w_qkv, preferred_element_type=jnp.float32).astype(jnp.bfloat16)
        query_heads = qkv[:, :model_width].reshape(blocks, F_DEV, HEADS, head_size).astype(jnp.float32)
        key_value = qkv[:, model_width:].reshape(blocks, F_DEV, 2 * model_width)
        previous = jnp.concatenate([jnp.zeros_like(key_value[:1]), key_value[:-1]], 0)
        kv_all = jnp.concatenate([previous, key_value], 1).astype(jnp.float32)
        key_heads = kv_all[..., :model_width].reshape(blocks, 2 * F_DEV, HEADS, head_size)
        value_heads = kv_all[..., model_width:].reshape(blocks, 2 * F_DEV, HEADS, head_size)
        scores = jnp.einsum("bfhd,bghd->bhfg", query_heads, key_heads, precision=hp) * score_scale
        block_ids = jnp.arange(blocks)
        columns = jnp.arange(2 * F_DEV)
        valid = jnp.logical_or((block_ids > 0)[:, None, None, None], (columns >= F_DEV)[None, None, None, :])
        scores = jnp.where(valid, scores, -1e30)
        peak = jnp.max(scores, axis=-1, keepdims=True)
        expo = jnp.exp(scores - peak)
        prob = expo / jnp.sum(expo, axis=-1, keepdims=True)
        prob_b = lax.optimization_barrier(prob.astype(jnp.bfloat16)).astype(jnp.float32)
        grad_heads = grad_one.reshape(blocks, F_DEV, HEADS, head_size).astype(jnp.float32)
        dprob = jnp.einsum("bfhd,bghd->bhfg", grad_heads, value_heads, precision=hp)
        delta = jnp.sum(prob * dprob, axis=-1, keepdims=True)
        dscore = lax.optimization_barrier((prob * (dprob - delta) * score_scale).astype(jnp.bfloat16)).astype(jnp.float32)
        grad_query = jnp.einsum("bhfg,bghd->bfhd", dscore, key_heads, precision=hp).astype(jnp.bfloat16)
        grad_key = jnp.einsum("bhfg,bfhd->bghd", dscore, query_heads, precision=hp)
        grad_value = jnp.einsum("bhfg,bfhd->bghd", prob_b, grad_heads, precision=hp)
        grad_kv = jnp.concatenate([grad_key.reshape(blocks, 2 * F_DEV, model_width), grad_value.reshape(blocks, 2 * F_DEV, model_width)], -1)
        earlier = grad_kv[:, :F_DEV]
        own_part = grad_kv[:, F_DEV:]
        summed = own_part + jnp.concatenate([earlier[1:], jnp.zeros_like(earlier[:1])], 0)
        grad_cat = jnp.concatenate([grad_query.reshape(frame_count, model_width), summed.astype(jnp.bfloat16).reshape(frame_count, 2 * model_width)], -1)
        grad_frames = jnp.dot(grad_cat, w_qkv.T, preferred_element_type=jnp.float32).astype(jnp.bfloat16)
        weight_part = jnp.dot(frames_one.T, grad_cat, preferred_element_type=jnp.float32)
        return grad_frames, weight_part

    grad_in, weight_parts = lax.map(one_record, (frames_in, grad_out))
    grad_w = jnp.sum(weight_parts, axis=0) * float(records * frame_count) ** -0.5
    return grad_in, grad_w
```

```python
import functools

import jax
import jax.numpy as jnp
from jax import lax
from jax.experimental import pallas as pl
from jax.experimental.pallas import tpu as pltpu
from jax.sharding import PartitionSpec as P

HEADS = 8
LOG2E = 1.4426950408889634
NT = (((1,), (1,)), ((), ()))
TN = (((0,), (0,)), ((), ()))


def passed_along(value, axis, steps):
    count = lax.axis_size(axis)
    first, last = (max(0, -steps), min(count, count - steps))
    return lax.ppermute(value, axis, [(source, source + steps) for source in range(first, last)])


def dot(a, b, dims=(((1,), (0,)), ((), ()))):
    return lax.dot_general(a, b, dims, preferred_element_type=jnp.float32)


def attention_kernel(width, qkv_ref, prev_ref, grad_ref, own_ref, earlier_ref):
    head_size = width // HEADS
    scale = head_size ** (-0.5)
    bias = jnp.where(lax.axis_index("tm") > 0, 0.0, -1e30).astype(jnp.float32)

    def columns(section):
        start = section * width + pl.program_id(0) * head_size
        return pl.ds(pl.multiple_of(start, head_size), head_size)

    q = qkv_ref[:, columns(0)]
    k_own = qkv_ref[:, columns(1)]
    v_own = qkv_ref[:, columns(2)]
    k_prev = prev_ref[:, columns(0)]
    v_prev = prev_ref[:, columns(1)]
    grad = grad_ref[:, columns(0)]
    s_own = dot(k_own, q, NT)
    s_prev = dot(k_prev, q, NT) + bias
    peak = jnp.maximum(jnp.max(s_own, 0, keepdims=True), jnp.max(s_prev, 0, keepdims=True))
    e_own = jnp.exp2((s_own - peak) * (scale * LOG2E))
    e_prev = jnp.exp2((s_prev - peak) * (scale * LOG2E))
    total = jnp.sum(e_own, 0, keepdims=True) + jnp.sum(e_prev, 0, keepdims=True)
    inverse = 1.0 / total
    p_own = e_own * inverse
    p_prev = e_prev * inverse
    dp_own = dot(v_own, grad, NT)
    dp_prev = dot(v_prev, grad, NT)
    delta = jnp.sum(p_own * dp_own, 0, keepdims=True) + jnp.sum(p_prev * dp_prev, 0, keepdims=True)
    ds_own = (p_own * (dp_own - delta)).astype(jnp.bfloat16)
    ds_prev = (p_prev * (dp_prev - delta)).astype(jnp.bfloat16)
    dq = dot(ds_own, k_own, TN) + dot(ds_prev, k_prev, TN)
    own_ref[:, columns(0)] = (dq * scale).astype(jnp.bfloat16)
    own_ref[:, columns(1)] = (dot(ds_own, q) * scale).astype(jnp.bfloat16)
    own_ref[:, columns(2)] = dot(p_own.astype(jnp.bfloat16), grad).astype(jnp.bfloat16)
    earlier_ref[:, columns(0)] = (dot(ds_prev, q) * scale).astype(jnp.bfloat16)
    earlier_ref[:, columns(1)] = dot(p_prev.astype(jnp.bfloat16), grad).astype(jnp.bfloat16)


def attention(qkv, prev, grad):
    frames, width = grad.shape
    whole = lambda a: pl.BlockSpec(a.shape, lambda h: (0, 0))
    outs = (
        jax.ShapeDtypeStruct((frames, 3 * width), jnp.bfloat16),
        jax.ShapeDtypeStruct((frames, 2 * width), jnp.bfloat16),
    )
    return pl.pallas_call(
        functools.partial(attention_kernel, width),
        grid=(HEADS,),
        in_specs=[whole(qkv), whole(prev), whole(grad)],
        out_specs=[whole(o) for o in outs],
        out_shape=outs,
        cost_estimate=pl.CostEstimate(
            flops=20 * frames * frames * width,
            bytes_accessed=22 * frames * width,
            transcendentals=2 * HEADS * frames * frames,
        ),
    )(qkv, prev, grad)


def local(frames_in, w_qkv, grad_out):
    records, frame_count, width = frames_in.shape
    w_kv = w_qkv[:, width:]
    total_frames = records * frame_count * lax.axis_size("stream") * lax.axis_size("tm")
    before = [passed_along(frames_in[r], "tm", 1) for r in range(records)]
    own_in, own, earlier, returned = [], [], [], []
    for r in range(records):
        qkv = dot(frames_in[r], w_qkv).astype(jnp.bfloat16)
        prev = dot(before[r], w_kv).astype(jnp.bfloat16)
        d_own, d_earlier = attention(qkv, prev, grad_out[r])
        back = dot(d_earlier, w_kv, NT).astype(jnp.bfloat16)
        returned.append(passed_along(back, "tm", -1))
        own.append(d_own)
        earlier.append(d_earlier)
    q_terms = sum(dot(frames_in[r], own[r][:, :width], TN) for r in range(records))
    kv_terms = sum(
        dot(frames_in[r], own[r][:, width:], TN) + dot(before[r], earlier[r], TN)
        for r in range(records)
    )
    terms = jnp.concatenate([q_terms, kv_terms], 1).astype(jnp.bfloat16)
    reduced = lax.psum_scatter(terms, ("stream", "tm"), scatter_dimension=0, tiled=True)
    grad_w = reduced.astype(jnp.float32) * float(total_frames) ** (-0.5)
    grad_in = jnp.stack(
        [
            (dot(own[r], w_qkv, NT) + returned[r].astype(jnp.float32)).astype(jnp.bfloat16)
            for r in range(records)
        ]
    )
    return (grad_in, grad_w)


def solution(mesh):
    return jax.shard_map(
        local,
        mesh=mesh,
        in_specs=(P("stream", "tm", None), P(), P("stream", "tm", None)),
        out_specs=(P("stream", "tm", None), P(("stream", "tm"), None)),
        check_vma=False,
    )
```

```python
import functools

import jax
import jax.numpy as jnp
from jax import lax
from jax.experimental import pallas as pl
from jax.experimental.pallas import tpu as pltpu
from jax.sharding import PartitionSpec as P

HEADS = 8
LOG2E = 1.4426950408889634
NT = (((1,), (1,)), ((), ()))
TN = (((0,), (0,)), ((), ()))


def passed_along(value, axis, steps):
    count = lax.axis_size(axis)
    first, last = (max(0, -steps), min(count, count - steps))
    return lax.ppermute(value, axis, [(source, source + steps) for source in range(first, last)])


def dot(a, b, dims=(((1,), (0,)), ((), ()))):
    return lax.dot_general(a, b, dims, preferred_element_type=jnp.float32)


def attention_kernel(width, qkv_ref, prev_ref, grad_ref, own_ref, earlier_ref):
    head_size = width // HEADS
    scale = head_size ** (-0.5)
    bias = jnp.where(lax.axis_index("tm") > 0, 0.0, -1e30).astype(jnp.float32)

    def columns(section):
        start = section * width + pl.program_id(0) * head_size
        return pl.ds(pl.multiple_of(start, head_size), head_size)

    q = qkv_ref[:, columns(0)]
    k_own = qkv_ref[:, columns(1)]
    v_own = qkv_ref[:, columns(2)]
    k_prev = prev_ref[:, columns(0)]
    v_prev = prev_ref[:, columns(1)]
    grad = grad_ref[:, columns(0)]
    s_own = dot(k_own, q, NT)
    s_prev = dot(k_prev, q, NT) + bias
    peak = jnp.maximum(jnp.max(s_own, 0, keepdims=True), jnp.max(s_prev, 0, keepdims=True))
    e_own = jnp.exp2((s_own - peak) * (scale * LOG2E))
    e_prev = jnp.exp2((s_prev - peak) * (scale * LOG2E))
    total = jnp.sum(e_own, 0, keepdims=True) + jnp.sum(e_prev, 0, keepdims=True)
    inverse = 1.0 / total
    p_own = e_own * inverse
    p_prev = e_prev * inverse
    dp_own = dot(v_own, grad, NT)
    dp_prev = dot(v_prev, grad, NT)
    delta = jnp.sum(p_own * dp_own, 0, keepdims=True) + jnp.sum(p_prev * dp_prev, 0, keepdims=True)
    ds_own = (p_own * (dp_own - delta)).astype(jnp.bfloat16)
    ds_prev = (p_prev * (dp_prev - delta)).astype(jnp.bfloat16)
    dq = dot(ds_own, k_own, TN) + dot(ds_prev, k_prev, TN)
    own_ref[:, columns(0)] = (dq * scale).astype(jnp.bfloat16)
    own_ref[:, columns(1)] = (dot(ds_own, q) * scale).astype(jnp.bfloat16)
    own_ref[:, columns(2)] = dot(p_own.astype(jnp.bfloat16), grad).astype(jnp.bfloat16)
    earlier_ref[:, columns(0)] = (dot(ds_prev, q) * scale).astype(jnp.bfloat16)
    earlier_ref[:, columns(1)] = dot(p_prev.astype(jnp.bfloat16), grad).astype(jnp.bfloat16)


def attention(qkv, prev, grad):
    frames, width = grad.shape
    whole = lambda a: pl.BlockSpec(a.shape, lambda h: (0, 0))
    outs = (
        jax.ShapeDtypeStruct((frames, 3 * width), jnp.bfloat16),
        jax.ShapeDtypeStruct((frames, 2 * width), jnp.bfloat16),
    )
    return pl.pallas_call(
        functools.partial(attention_kernel, width),
        grid=(HEADS,),
        in_specs=[whole(qkv), whole(prev), whole(grad)],
        out_specs=[whole(o) for o in outs],
        out_shape=outs,
        cost_estimate=pl.CostEstimate(
            flops=20 * frames * frames * width,
            bytes_accessed=22 * frames * width,
            transcendentals=2 * HEADS * frames * frames,
        ),
    )(qkv, prev, grad)


def bit_of(index, bit):
    return (index // (1 << bit)) % 2


def reduce_kernel(records, scale, *refs):
    frames, before = refs[:records], refs[records : 2 * records]
    own, earlier = refs[2 * records : 3 * records], refs[3 * records : 4 * records]
    out_ref, held, landed, send_sem, recv_sem = refs[4 * records :]
    width = frames[0].shape[1]
    streams, blocks = lax.axis_size("stream"), lax.axis_size("tm")
    stream, block = lax.axis_index("stream"), lax.axis_index("tm")
    stream_bits, block_bits = streams.bit_length() - 1, blocks.bit_length() - 1
    dims = [("stream", b, bit_of(stream, b)) for b in reversed(range(stream_bits))]
    dims += [("tm", b, bit_of(block, b)) for b in reversed(range(block_bits))]
    count = len(dims)
    first = stream_bits - 1
    rest = list(reversed(range(first))) + list(reversed(range(first + 1, count)))
    orders = [[first] + rest[c % len(rest) :] + rest[: c % len(rest)] for c in range(3)]

    def partner(d):
        axis, b, value = dims[d]
        return {axis: (stream if axis == "stream" else block) + (1 - 2 * value) * (1 << b)}

    barrier = pltpu.get_barrier_semaphore()
    for d in range(count):
        pl.semaphore_signal(
            barrier, inc=1, device_id=partner(d), device_id_type=pl.DeviceIdType.MESH
        )
    pl.semaphore_wait(barrier, count)

    rows = width // streams

    def products(parity):
        def body(j, carry):
            piece = 2 * j + parity
            span = pl.ds(pl.multiple_of(piece * rows, rows), rows)
            lead = [bit_of(piece, b) for b in reversed(range(stream_bits))]
            for c in range(3):
                total = 0.0
                for r in range(records):
                    cols = slice(c * width, (c + 1) * width)
                    total += dot(frames[r][:, span], own[r][:, cols], TN)
                    if c > 0:
                        cols = slice((c - 1) * width, c * width)
                        total += dot(before[r][:, span], earlier[r][:, cols], TN)
                shape = held.shape[1 + stream_bits :]
                held[(c, *lead)] = total.astype(held.dtype).reshape(shape)
            return carry

        lax.fori_loop(0, streams // 2, body, 0)

    def region(c, phase, kept):
        index = [slice(None)] * count
        for d in orders[c][:phase]:
            index[d] = dims[d][2]
        last = orders[c][phase]
        index[last] = dims[last][2] if kept else 1 - dims[last][2]
        return (c, *index)

    def copy(c, phase):
        return pltpu.make_async_remote_copy(
            src_ref=held.at[region(c, phase, False)],
            dst_ref=landed.at[region(c, phase, True)],
            send_sem=send_sem.at[c, phase],
            recv_sem=recv_sem.at[c, phase],
            device_id=partner(orders[c][phase]),
            device_id_type=pl.DeviceIdType.MESH,
        )

    def merge(c, phase):
        free = [d for d in range(count) if d not in orders[c][: phase + 1]]

        def body(j, carry):
            kept = list(region(c, phase, True))
            arrived = list(region(c, phase, False))
            for k, d in enumerate(free):
                kept[1 + d] = arrived[1 + d] = bit_of(j, k)
            kept, arrived = tuple(kept), tuple(arrived)
            total = held[kept].astype(jnp.float32) + landed[arrived].astype(jnp.float32)
            if free:
                held[kept] = total.astype(held.dtype)
            else:
                out_ref[:, c * width : (c + 1) * width] = total * scale
            return carry

        if free:
            lax.fori_loop(0, 1 << len(free), body, 0)
        else:
            body(0, 0)

    products(1 - dims[first][2])
    for c in range(3):
        copy(c, 0).start()
    products(dims[first][2])
    for phase in range(count):
        for c in range(3):
            copy(c, phase).wait_recv()
            merge(c, phase)
            if phase + 1 < count:
                copy(c, phase + 1).start()
    for phase in range(count):
        for c in range(3):
            copy(c, phase).wait_send()


def weight_gradient(frames, before, own, earlier, scale):
    records = len(frames)
    width = frames[0].shape[1]
    devices = lax.axis_size("stream") * lax.axis_size("tm")
    count = devices.bit_length() - 1
    part = pltpu.VMEM((3, *([2] * count), width // devices, width), jnp.bfloat16)
    operands = (*frames, *before, *own, *earlier)
    return pl.pallas_call(
        functools.partial(reduce_kernel, records, scale),
        in_specs=[pl.BlockSpec(memory_space=pltpu.VMEM)] * len(operands),
        out_specs=pl.BlockSpec(memory_space=pltpu.VMEM),
        out_shape=jax.ShapeDtypeStruct((width // devices, 3 * width), jnp.float32),
        scratch_shapes=[
            part,
            part,
            pltpu.SemaphoreType.DMA((3, count)),
            pltpu.SemaphoreType.DMA((3, count)),
        ],
        compiler_params=pltpu.CompilerParams(collective_id=0, has_side_effects=True),
        cost_estimate=pl.CostEstimate(
            flops=100 * records * frames[0].size * width // 10,
            bytes_accessed=22 * records * frames[0].size,
            transcendentals=0,
        ),
    )(*operands)


def local(frames_in, w_qkv, grad_out):
    records, frame_count, width = frames_in.shape
    w_kv = w_qkv[:, width:]
    total_frames = records * frame_count * lax.axis_size("stream") * lax.axis_size("tm")
    before = [passed_along(frames_in[r], "tm", 1) for r in range(records)]
    own, earlier, returned = [], [], []
    for r in range(records):
        qkv = dot(frames_in[r], w_qkv).astype(jnp.bfloat16)
        prev = dot(before[r], w_kv).astype(jnp.bfloat16)
        d_own, d_earlier = attention(qkv, prev, grad_out[r])
        back = dot(d_earlier, w_kv, NT).astype(jnp.bfloat16)
        returned.append(passed_along(back, "tm", -1))
        own.append(d_own)
        earlier.append(d_earlier)
    grad_w = weight_gradient(
        [frames_in[r] for r in range(records)],
        before,
        own,
        earlier,
        float(total_frames) ** (-0.5),
    )
    grad_in = jnp.stack(
        [
            (dot(own[r], w_qkv, NT) + returned[r].astype(jnp.float32)).astype(jnp.bfloat16)
            for r in range(records)
        ]
    )
    return (grad_in, grad_w)


def solution(mesh):
    return jax.shard_map(
        local,
        mesh=mesh,
        in_specs=(P("stream", "tm", None), P(), P("stream", "tm", None)),
        out_specs=(P("stream", "tm", None), P(("stream", "tm"), None)),
        check_vma=False,
    )
```

```python
import functools

import jax
import jax.numpy as jnp
from jax import lax
from jax.experimental import pallas as pl
from jax.experimental.pallas import tpu as pltpu
from jax.sharding import PartitionSpec as P

HEADS = 8
LOG2E = 1.4426950408889634
NT = (((1,), (1,)), ((), ()))
TN = (((0,), (0,)), ((), ()))


def passed_along(value, axis, steps):
    count = lax.axis_size(axis)
    first, last = (max(0, -steps), min(count, count - steps))
    return lax.ppermute(value, axis, [(source, source + steps) for source in range(first, last)])


def dot(a, b, dims=(((1,), (0,)), ((), ()))):
    return lax.dot_general(a, b, dims, preferred_element_type=jnp.float32)


def attention_kernel(width, qkv_ref, prev_ref, grad_ref, own_ref, earlier_ref):
    head_size = width // HEADS
    scale = head_size ** (-0.5)
    bias = jnp.where(lax.axis_index("tm") > 0, 0.0, -1e30).astype(jnp.float32)

    def columns(section):
        start = section * width + pl.program_id(0) * head_size
        return pl.ds(pl.multiple_of(start, head_size), head_size)

    q = qkv_ref[:, columns(0)]
    k_own = qkv_ref[:, columns(1)]
    v_own = qkv_ref[:, columns(2)]
    k_prev = prev_ref[:, columns(0)]
    v_prev = prev_ref[:, columns(1)]
    grad = grad_ref[:, columns(0)]
    s_own = dot(k_own, q, NT)
    s_prev = dot(k_prev, q, NT) + bias
    peak = jnp.maximum(jnp.max(s_own, 0, keepdims=True), jnp.max(s_prev, 0, keepdims=True))
    e_own = jnp.exp2((s_own - peak) * (scale * LOG2E))
    e_prev = jnp.exp2((s_prev - peak) * (scale * LOG2E))
    total = jnp.sum(e_own, 0, keepdims=True) + jnp.sum(e_prev, 0, keepdims=True)
    inverse = 1.0 / total
    p_own = e_own * inverse
    p_prev = e_prev * inverse
    dp_own = dot(v_own, grad, NT)
    dp_prev = dot(v_prev, grad, NT)
    delta = jnp.sum(p_own * dp_own, 0, keepdims=True) + jnp.sum(p_prev * dp_prev, 0, keepdims=True)
    ds_own = (p_own * (dp_own - delta)).astype(jnp.bfloat16)
    ds_prev = (p_prev * (dp_prev - delta)).astype(jnp.bfloat16)
    dq = dot(ds_own, k_own, TN) + dot(ds_prev, k_prev, TN)
    own_ref[:, columns(0)] = (dq * scale).astype(jnp.bfloat16)
    own_ref[:, columns(1)] = (dot(ds_own, q) * scale).astype(jnp.bfloat16)
    own_ref[:, columns(2)] = dot(p_own.astype(jnp.bfloat16), grad).astype(jnp.bfloat16)
    earlier_ref[:, columns(0)] = (dot(ds_prev, q) * scale).astype(jnp.bfloat16)
    earlier_ref[:, columns(1)] = dot(p_prev.astype(jnp.bfloat16), grad).astype(jnp.bfloat16)


def attention(qkv, prev, grad):
    frames, width = grad.shape
    whole = lambda a: pl.BlockSpec(a.shape, lambda h: (0, 0))
    outs = (
        jax.ShapeDtypeStruct((frames, 3 * width), jnp.bfloat16),
        jax.ShapeDtypeStruct((frames, 2 * width), jnp.bfloat16),
    )
    return pl.pallas_call(
        functools.partial(attention_kernel, width),
        grid=(HEADS,),
        in_specs=[whole(qkv), whole(prev), whole(grad)],
        out_specs=[whole(o) for o in outs],
        out_shape=outs,
        cost_estimate=pl.CostEstimate(
            flops=20 * frames * frames * width,
            bytes_accessed=22 * frames * width,
            transcendentals=2 * HEADS * frames * frames,
        ),
    )(qkv, prev, grad)


def bit_of(index, bit):
    return (index // (1 << bit)) % 2


def reduce_kernel(records, scale, *refs):
    frames, before = refs[:records], refs[records : 2 * records]
    own, earlier = refs[2 * records : 3 * records], refs[3 * records : 4 * records]
    returned, w_ref = refs[4 * records : 5 * records - 1], refs[5 * records - 1]
    out_ref, grad_ref, held, landed, sums, leaving, arriving = refs[5 * records : 5 * records + 7]
    send_sem, recv_sem, back_send_sem, back_recv_sem = refs[5 * records + 7 :]
    width = frames[0].shape[1]
    streams, blocks = lax.axis_size("stream"), lax.axis_size("tm")
    stream, block = lax.axis_index("stream"), lax.axis_index("tm")
    stream_bits, block_bits = streams.bit_length() - 1, blocks.bit_length() - 1
    dims = [("stream", b, bit_of(stream, b)) for b in reversed(range(stream_bits))]
    dims += [("tm", b, bit_of(block, b)) for b in reversed(range(block_bits))]
    count = len(dims)
    first = stream_bits - 1
    rest = list(reversed(range(first))) + list(reversed(range(first + 1, count)))
    orders = [[first] + rest[c % len(rest) :] + rest[: c % len(rest)] for c in range(3)]

    def partner(d):
        axis, b, value = dims[d]
        return {axis: (stream if axis == "stream" else block) + (1 - 2 * value) * (1 << b)}

    barrier = pltpu.get_barrier_semaphore()
    for d in range(count):
        pl.semaphore_signal(
            barrier, inc=1, device_id=partner(d), device_id_type=pl.DeviceIdType.MESH
        )
    has_before, has_after = block > 0, block < blocks - 1

    def greet(step):
        pl.semaphore_signal(
            barrier,
            inc=1,
            device_id={"tm": block + step},
            device_id_type=pl.DeviceIdType.MESH,
        )

    pl.when(has_before)(lambda: greet(-1))
    pl.when(has_after)(lambda: greet(1))
    beside = (block + blocks - 1) // blocks + (2 * blocks - 2 - block) // blocks
    pl.semaphore_wait(barrier, count + beside)
    back = pltpu.make_async_remote_copy(
        src_ref=leaving,
        dst_ref=arriving,
        send_sem=back_send_sem,
        recv_sem=back_recv_sem,
        device_id={"tm": block - 1},
        device_id_type=pl.DeviceIdType.MESH,
    )

    def by_columns(store):
        step = 256

        def body(j, carry):
            span = pl.ds(pl.multiple_of(j * step, step), step)
            store(span)
            return carry

        lax.fori_loop(0, width // step, body, 0)

    def returning(span):
        terms = dot(earlier[-1][...], w_ref[span, width:], NT)
        leaving[:, span] = terms.astype(leaving.dtype)

    def own_terms(r, span):
        terms = dot(own[r][...], w_ref[span, :], NT)
        if r < records - 1:
            terms += returned[r][:, span].astype(jnp.float32)
            grad_ref[r, :, span] = terms.astype(grad_ref.dtype)
        else:
            sums[:, span] = terms

    work = [functools.partial(by_columns, functools.partial(own_terms, r)) for r in range(records)]

    rows = width // streams

    def products(parity):
        def body(j, carry):
            piece = 2 * j + parity
            span = pl.ds(pl.multiple_of(piece * rows, rows), rows)
            lead = [bit_of(piece, b) for b in reversed(range(stream_bits))]
            for c in range(3):
                total = 0.0
                for r in range(records):
                    cols = slice(c * width, (c + 1) * width)
                    total += dot(frames[r][:, span], own[r][:, cols], TN)
                    if c > 0:
                        cols = slice((c - 1) * width, c * width)
                        total += dot(before[r][:, span], earlier[r][:, cols], TN)
                shape = held.shape[1 + stream_bits :]
                held[(c, *lead)] = total.astype(held.dtype).reshape(shape)
            return carry

        lax.fori_loop(0, streams // 2, body, 0)

    def region(c, phase, kept):
        index = [slice(None)] * count
        for d in orders[c][:phase]:
            index[d] = dims[d][2]
        last = orders[c][phase]
        index[last] = dims[last][2] if kept else 1 - dims[last][2]
        return (c, *index)

    def copy(c, phase):
        return pltpu.make_async_remote_copy(
            src_ref=held.at[region(c, phase, False)],
            dst_ref=landed.at[region(c, phase, True)],
            send_sem=send_sem.at[c, phase],
            recv_sem=recv_sem.at[c, phase],
            device_id=partner(orders[c][phase]),
            device_id_type=pl.DeviceIdType.MESH,
        )

    def merge(c, phase):
        free = [d for d in range(count) if d not in orders[c][: phase + 1]]

        def body(j, carry):
            kept = list(region(c, phase, True))
            arrived = list(region(c, phase, False))
            for k, d in enumerate(free):
                kept[1 + d] = arrived[1 + d] = bit_of(j, k)
            kept, arrived = tuple(kept), tuple(arrived)
            total = held[kept].astype(jnp.float32) + landed[arrived].astype(jnp.float32)
            if free:
                held[kept] = total.astype(held.dtype)
            else:
                out_ref[:, c * width : (c + 1) * width] = total * scale
            return carry

        if free:
            lax.fori_loop(0, 1 << len(free), body, 0)
        else:
            body(0, 0)

    by_columns(returning)
    pl.when(has_before)(back.start)
    products(1 - dims[first][2])
    for c in range(3):
        copy(c, 0).start()
    products(dims[first][2])
    for phase in range(count):
        if 0 < phase <= records:
            work[phase - 1]()
        for c in range(3):
            copy(c, phase).wait_recv()
            merge(c, phase)
            if phase + 1 < count:
                copy(c, phase + 1).start()
    for phase in range(count):
        for c in range(3):
            copy(c, phase).wait_send()
    pl.when(has_before)(back.wait_send)
    last = records - 1

    @pl.when(has_after)
    def _():
        back.wait_recv()
        grad_ref[last] = (sums[...] + arriving[...].astype(jnp.float32)).astype(grad_ref.dtype)

    @pl.when(jnp.logical_not(has_after))
    def _():
        grad_ref[last] = sums[...].astype(grad_ref.dtype)


def gradients(frames, before, own, earlier, returned, w_qkv, scale):
    records = len(frames)
    rows, width = frames[0].shape
    devices = lax.axis_size("stream") * lax.axis_size("tm")
    count = devices.bit_length() - 1
    part = pltpu.VMEM((3, *([2] * count), width // devices, width), jnp.bfloat16)
    operands = (*frames, *before, *own, *earlier, *returned, w_qkv)
    return pl.pallas_call(
        functools.partial(reduce_kernel, records, scale),
        in_specs=[pl.BlockSpec(memory_space=pltpu.VMEM)] * len(operands),
        out_specs=[pl.BlockSpec(memory_space=pltpu.VMEM)] * 2,
        out_shape=(
            jax.ShapeDtypeStruct((width // devices, 3 * width), jnp.float32),
            jax.ShapeDtypeStruct((records, rows, width), jnp.bfloat16),
        ),
        scratch_shapes=[
            part,
            part,
            pltpu.VMEM((rows, width), jnp.float32),
            pltpu.VMEM((rows, width), jnp.bfloat16),
            pltpu.VMEM((rows, width), jnp.bfloat16),
            pltpu.SemaphoreType.DMA((3, count)),
            pltpu.SemaphoreType.DMA((3, count)),
            pltpu.SemaphoreType.DMA,
            pltpu.SemaphoreType.DMA,
        ],
        compiler_params=pltpu.CompilerParams(collective_id=0, has_side_effects=True),
        cost_estimate=pl.CostEstimate(
            flops=20 * records * frames[0].size * width,
            bytes_accessed=22 * records * frames[0].size,
            transcendentals=0,
        ),
    )(*operands)


def local(frames_in, w_qkv, grad_out):
    records, frame_count, width = frames_in.shape
    w_kv = w_qkv[:, width:]
    total_frames = records * frame_count * lax.axis_size("stream") * lax.axis_size("tm")
    before = [passed_along(frames_in[r], "tm", 1) for r in range(records)]
    own, earlier, returned = [], [], []
    for r in range(records):
        qkv = dot(frames_in[r], w_qkv).astype(jnp.bfloat16)
        prev = dot(before[r], w_kv).astype(jnp.bfloat16)
        d_own, d_earlier = attention(qkv, prev, grad_out[r])
        if r < records - 1:
            back = dot(d_earlier, w_kv, NT).astype(jnp.bfloat16)
            returned.append(passed_along(back, "tm", -1))
        own.append(d_own)
        earlier.append(d_earlier)
    grad_w, grad_in = gradients(
        [frames_in[r] for r in range(records)],
        before,
        own,
        earlier,
        returned,
        w_qkv,
        float(total_frames) ** (-0.5),
    )
    return (grad_in, grad_w)


def solution(mesh):
    return jax.shard_map(
        local,
        mesh=mesh,
        in_specs=(P("stream", "tm", None), P(), P("stream", "tm", None)),
        out_specs=(P("stream", "tm", None), P(("stream", "tm"), None)),
        check_vma=False,
    )
```

```python
import functools

import jax
import jax.numpy as jnp
from jax import lax
from jax.experimental import pallas as pl
from jax.experimental.pallas import tpu as pltpu
from jax.sharding import PartitionSpec as P

HEADS = 8
TOGETHER = 2
LOG2E = 1.4426950408889634
NT = (((1,), (1,)), ((), ()))
TN = (((0,), (0,)), ((), ()))


def passed_along(value, axis, steps):
    count = lax.axis_size(axis)
    first, last = (max(0, -steps), min(count, count - steps))
    return lax.ppermute(value, axis, [(source, source + steps) for source in range(first, last)])


def dot(a, b, dims=(((1,), (0,)), ((), ()))):
    return lax.dot_general(a, b, dims, preferred_element_type=jnp.float32)


def attention_kernel(width, qkv_ref, prev_ref, grad_ref, own_ref, earlier_ref):
    head_size = width // HEADS
    scale = head_size ** (-0.5)
    bias = jnp.where(lax.axis_index("tm") > 0, 0.0, -1e30).astype(jnp.float32)

    def one_head(turn):
        def columns(section):
            start = section * width + (pl.program_id(0) * TOGETHER + turn) * head_size
            return pl.ds(pl.multiple_of(start, head_size), head_size)

        q = qkv_ref[:, columns(0)]
        k_own = qkv_ref[:, columns(1)]
        v_own = qkv_ref[:, columns(2)]
        k_prev = prev_ref[:, columns(0)]
        v_prev = prev_ref[:, columns(1)]
        grad = grad_ref[:, columns(0)]
        s_own = dot(k_own, q, NT)
        s_prev = dot(k_prev, q, NT) + bias
        peak = jnp.maximum(jnp.max(s_own, 0, keepdims=True), jnp.max(s_prev, 0, keepdims=True))
        e_own = jnp.exp2((s_own - peak) * (scale * LOG2E))
        e_prev = jnp.exp2((s_prev - peak) * (scale * LOG2E))
        total = jnp.sum(e_own, 0, keepdims=True) + jnp.sum(e_prev, 0, keepdims=True)
        inverse = 1.0 / total
        p_own = e_own * inverse
        p_prev = e_prev * inverse
        dp_own = dot(v_own, grad, NT)
        dp_prev = dot(v_prev, grad, NT)
        delta = jnp.sum(p_own * dp_own, 0, keepdims=True) + jnp.sum(p_prev * dp_prev, 0, keepdims=True)
        ds_own = (p_own * (dp_own - delta)).astype(jnp.bfloat16)
        ds_prev = (p_prev * (dp_prev - delta)).astype(jnp.bfloat16)
        dq = dot(ds_own, k_own, TN) + dot(ds_prev, k_prev, TN)
        own_ref[:, columns(0)] = (dq * scale).astype(jnp.bfloat16)
        own_ref[:, columns(1)] = (dot(ds_own, q) * scale).astype(jnp.bfloat16)
        own_ref[:, columns(2)] = dot(p_own.astype(jnp.bfloat16), grad).astype(jnp.bfloat16)
        earlier_ref[:, columns(0)] = (dot(ds_prev, q) * scale).astype(jnp.bfloat16)
        earlier_ref[:, columns(1)] = dot(p_prev.astype(jnp.bfloat16), grad).astype(jnp.bfloat16)

    for turn in range(TOGETHER):
        one_head(turn)


def attention(qkv, prev, grad):
    frames, width = grad.shape
    whole = lambda a: pl.BlockSpec(a.shape, lambda h: (0, 0))
    outs = (
        jax.ShapeDtypeStruct((frames, 3 * width), jnp.bfloat16),
        jax.ShapeDtypeStruct((frames, 2 * width), jnp.bfloat16),
    )
    return pl.pallas_call(
        functools.partial(attention_kernel, width),
        grid=(HEADS // TOGETHER,),
        in_specs=[whole(qkv), whole(prev), whole(grad)],
        out_specs=[whole(o) for o in outs],
        out_shape=outs,
        cost_estimate=pl.CostEstimate(
            flops=20 * frames * frames * width,
            bytes_accessed=22 * frames * width,
            transcendentals=2 * HEADS * frames * frames,
        ),
    )(qkv, prev, grad)


def bit_of(index, bit):
    return (index // (1 << bit)) % 2


def reduce_kernel(records, scale, *refs):
    frames, before = refs[:records], refs[records : 2 * records]
    own, earlier = refs[2 * records : 3 * records], refs[3 * records : 4 * records]
    returned, w_ref = refs[4 * records : 5 * records - 1], refs[5 * records - 1]
    out_ref, grad_ref, held, landed, sums, leaving, arriving = refs[5 * records : 5 * records + 7]
    send_sem, recv_sem, back_send_sem, back_recv_sem = refs[5 * records + 7 :]
    width = frames[0].shape[1]
    streams, blocks = lax.axis_size("stream"), lax.axis_size("tm")
    stream, block = lax.axis_index("stream"), lax.axis_index("tm")
    stream_bits, block_bits = streams.bit_length() - 1, blocks.bit_length() - 1
    dims = [("stream", b, bit_of(stream, b)) for b in reversed(range(stream_bits))]
    dims += [("tm", b, bit_of(block, b)) for b in reversed(range(block_bits))]
    count = len(dims)
    first = stream_bits - 1
    rest = list(reversed(range(first))) + list(reversed(range(first + 1, count)))
    orders = [[first] + rest[c % len(rest) :] + rest[: c % len(rest)] for c in range(3)]

    def partner(d):
        axis, b, value = dims[d]
        return {axis: (stream if axis == "stream" else block) + (1 - 2 * value) * (1 << b)}

    barrier = pltpu.get_barrier_semaphore()
    for d in range(count):
        pl.semaphore_signal(
            barrier, inc=1, device_id=partner(d), device_id_type=pl.DeviceIdType.MESH
        )
    has_before, has_after = block > 0, block < blocks - 1

    def greet(step):
        pl.semaphore_signal(
            barrier,
            inc=1,
            device_id={"tm": block + step},
            device_id_type=pl.DeviceIdType.MESH,
        )

    pl.when(has_before)(lambda: greet(-1))
    pl.when(has_after)(lambda: greet(1))
    beside = (block + blocks - 1) // blocks + (2 * blocks - 2 - block) // blocks
    pl.semaphore_wait(barrier, count + beside)
    back = pltpu.make_async_remote_copy(
        src_ref=leaving,
        dst_ref=arriving,
        send_sem=back_send_sem,
        recv_sem=back_recv_sem,
        device_id={"tm": block - 1},
        device_id_type=pl.DeviceIdType.MESH,
    )

    def by_columns(store):
        step = 256

        def body(j, carry):
            span = pl.ds(pl.multiple_of(j * step, step), step)
            store(span)
            return carry

        lax.fori_loop(0, width // step, body, 0)

    def returning(span):
        terms = dot(earlier[-1][...], w_ref[span, width:], NT)
        leaving[:, span] = terms.astype(leaving.dtype)

    def own_terms(r, span):
        terms = dot(own[r][...], w_ref[span, :], NT)
        if r < records - 1:
            terms += returned[r][:, span].astype(jnp.float32)
            grad_ref[r, :, span] = terms.astype(grad_ref.dtype)
        else:
            sums[:, span] = terms

    work = [functools.partial(by_columns, functools.partial(own_terms, r)) for r in range(records)]

    rows = width // streams

    def products(parity):
        def body(j, carry):
            piece = 2 * j + parity
            span = pl.ds(pl.multiple_of(piece * rows, rows), rows)
            lead = [bit_of(piece, b) for b in reversed(range(stream_bits))]
            for c in range(3):
                total = 0.0
                for r in range(records):
                    cols = slice(c * width, (c + 1) * width)
                    total += dot(frames[r][:, span], own[r][:, cols], TN)
                    if c > 0:
                        cols = slice((c - 1) * width, c * width)
                        total += dot(before[r][:, span], earlier[r][:, cols], TN)
                shape = held.shape[1 + stream_bits :]
                held[(c, *lead)] = total.astype(held.dtype).reshape(shape)
            return carry

        lax.fori_loop(0, streams // 2, body, 0)

    def region(c, phase, kept):
        index = [slice(None)] * count
        for d in orders[c][:phase]:
            index[d] = dims[d][2]
        last = orders[c][phase]
        index[last] = dims[last][2] if kept else 1 - dims[last][2]
        return (c, *index)

    def copy(c, phase):
        return pltpu.make_async_remote_copy(
            src_ref=held.at[region(c, phase, False)],
            dst_ref=landed.at[region(c, phase, True)],
            send_sem=send_sem.at[c, phase],
            recv_sem=recv_sem.at[c, phase],
            device_id=partner(orders[c][phase]),
            device_id_type=pl.DeviceIdType.MESH,
        )

    def merge(c, phase):
        free = [d for d in range(count) if d not in orders[c][: phase + 1]]

        def body(j, carry):
            kept = list(region(c, phase, True))
            arrived = list(region(c, phase, False))
            for k, d in enumerate(free):
                kept[1 + d] = arrived[1 + d] = bit_of(j, k)
            kept, arrived = tuple(kept), tuple(arrived)
            total = held[kept].astype(jnp.float32) + landed[arrived].astype(jnp.float32)
            if free:
                held[kept] = total.astype(held.dtype)
            else:
                out_ref[:, c * width : (c + 1) * width] = total * scale
            return carry

        if free:
            lax.fori_loop(0, 1 << len(free), body, 0)
        else:
            body(0, 0)

    by_columns(returning)
    pl.when(has_before)(back.start)
    products(1 - dims[first][2])
    for c in range(3):
        copy(c, 0).start()
    products(dims[first][2])
    for phase in range(count):
        if 0 < phase <= records:
            work[phase - 1]()
        for c in range(3):
            copy(c, phase).wait_recv()
            merge(c, phase)
            if phase + 1 < count:
                copy(c, phase + 1).start()
    for phase in range(count):
        for c in range(3):
            copy(c, phase).wait_send()
    pl.when(has_before)(back.wait_send)
    last = records - 1

    @pl.when(has_after)
    def _():
        back.wait_recv()
        grad_ref[last] = (sums[...] + arriving[...].astype(jnp.float32)).astype(grad_ref.dtype)

    @pl.when(jnp.logical_not(has_after))
    def _():
        grad_ref[last] = sums[...].astype(grad_ref.dtype)


def gradients(frames, before, own, earlier, returned, w_qkv, scale):
    records = len(frames)
    rows, width = frames[0].shape
    devices = lax.axis_size("stream") * lax.axis_size("tm")
    count = devices.bit_length() - 1
    part = pltpu.VMEM((3, *([2] * count), width // devices, width), jnp.bfloat16)
    operands = (*frames, *before, *own, *earlier, *returned, w_qkv)
    return pl.pallas_call(
        functools.partial(reduce_kernel, records, scale),
        in_specs=[pl.BlockSpec(memory_space=pltpu.VMEM)] * len(operands),
        out_specs=[pl.BlockSpec(memory_space=pltpu.VMEM)] * 2,
        out_shape=(
            jax.ShapeDtypeStruct((width // devices, 3 * width), jnp.float32),
            jax.ShapeDtypeStruct((records, rows, width), jnp.bfloat16),
        ),
        scratch_shapes=[
            part,
            part,
            pltpu.VMEM((rows, width), jnp.float32),
            pltpu.VMEM((rows, width), jnp.bfloat16),
            pltpu.VMEM((rows, width), jnp.bfloat16),
            pltpu.SemaphoreType.DMA((3, count)),
            pltpu.SemaphoreType.DMA((3, count)),
            pltpu.SemaphoreType.DMA,
            pltpu.SemaphoreType.DMA,
        ],
        compiler_params=pltpu.CompilerParams(collective_id=0, has_side_effects=True),
        cost_estimate=pl.CostEstimate(
            flops=20 * records * frames[0].size * width,
            bytes_accessed=22 * records * frames[0].size,
            transcendentals=0,
        ),
    )(*operands)


def local(frames_in, w_qkv, grad_out):
    records, frame_count, width = frames_in.shape
    w_kv = w_qkv[:, width:]
    total_frames = records * frame_count * lax.axis_size("stream") * lax.axis_size("tm")
    before = [passed_along(frames_in[r], "tm", 1) for r in range(records)]
    own, earlier, returned = [], [], []
    joined = [dot(frames_in[r], w_qkv).astype(jnp.bfloat16) for r in range(records)]
    before[0], *joined = lax.optimization_barrier((before[0], *joined))
    for r in range(records):
        prev = dot(before[r], w_kv).astype(jnp.bfloat16)
        d_own, d_earlier = attention(joined[r], prev, grad_out[r])
        if r < records - 1:
            back = dot(d_earlier, w_kv, NT).astype(jnp.bfloat16)
            returned.append(passed_along(back, "tm", -1))
        own.append(d_own)
        earlier.append(d_earlier)
    grad_w, grad_in = gradients(
        [frames_in[r] for r in range(records)],
        before,
        own,
        earlier,
        returned,
        w_qkv,
        float(total_frames) ** (-0.5),
    )
    return (grad_in, grad_w)


def solution(mesh):
    return jax.shard_map(
        local,
        mesh=mesh,
        in_specs=(P("stream", "tm", None), P(), P("stream", "tm", None)),
        out_specs=(P("stream", "tm", None), P(("stream", "tm"), None)),
        check_vma=False,
    )
```

```python
import functools

import jax
import jax.numpy as jnp
from jax import lax
from jax.experimental import pallas as pl
from jax.experimental.pallas import tpu as pltpu
from jax.sharding import PartitionSpec as P

HEADS = 8
TOGETHER = 2
LOG2E = 1.4426950408889634
NT = (((1,), (1,)), ((), ()))
TN = (((0,), (0,)), ((), ()))


def passed_along(value, axis, steps):
    count = lax.axis_size(axis)
    first, last = (max(0, -steps), min(count, count - steps))
    return lax.ppermute(value, axis, [(source, source + steps) for source in range(first, last)])


def dot(a, b, dims=(((1,), (0,)), ((), ()))):
    return lax.dot_general(a, b, dims, preferred_element_type=jnp.float32)


def attention_kernel(width, qkv_ref, prev_ref, grad_ref, own_ref, earlier_ref):
    head_size = width // HEADS
    scale = head_size ** (-0.5)
    bias = jnp.where(lax.axis_index("tm") > 0, 0.0, -1e30).astype(jnp.float32)

    def one_head(turn):
        def columns(section):
            start = section * width + (pl.program_id(0) * TOGETHER + turn) * head_size
            return pl.ds(pl.multiple_of(start, head_size), head_size)

        q = qkv_ref[:, columns(0)]
        k_own = qkv_ref[:, columns(1)]
        v_own = qkv_ref[:, columns(2)]
        k_prev = prev_ref[:, columns(0)]
        v_prev = prev_ref[:, columns(1)]
        grad = grad_ref[:, columns(0)]
        s_own = dot(k_own, q, NT)
        s_prev = dot(k_prev, q, NT) + bias
        peak = jnp.maximum(jnp.max(s_own, 0, keepdims=True), jnp.max(s_prev, 0, keepdims=True))
        e_own = jnp.exp2((s_own - peak) * (scale * LOG2E))
        e_prev = jnp.exp2((s_prev - peak) * (scale * LOG2E))
        total = jnp.sum(e_own, 0, keepdims=True) + jnp.sum(e_prev, 0, keepdims=True)
        inverse = 1.0 / total
        p_own = e_own * inverse
        p_prev = e_prev * inverse
        dp_own = dot(v_own, grad, NT)
        dp_prev = dot(v_prev, grad, NT)
        delta = jnp.sum(p_own * dp_own, 0, keepdims=True) + jnp.sum(p_prev * dp_prev, 0, keepdims=True)
        ds_own = (p_own * (dp_own - delta)).astype(jnp.bfloat16)
        ds_prev = (p_prev * (dp_prev - delta)).astype(jnp.bfloat16)
        dq = dot(ds_own, k_own, TN) + dot(ds_prev, k_prev, TN)
        own_ref[:, columns(0)] = (dq * scale).astype(jnp.bfloat16)
        own_ref[:, columns(1)] = (dot(ds_own, q) * scale).astype(jnp.bfloat16)
        own_ref[:, columns(2)] = dot(p_own.astype(jnp.bfloat16), grad).astype(jnp.bfloat16)
        earlier_ref[:, columns(0)] = (dot(ds_prev, q) * scale).astype(jnp.bfloat16)
        earlier_ref[:, columns(1)] = dot(p_prev.astype(jnp.bfloat16), grad).astype(jnp.bfloat16)

    for turn in range(TOGETHER):
        one_head(turn)


def attention(qkv, prev, grad):
    frames, width = grad.shape
    whole = lambda a: pl.BlockSpec(a.shape, lambda h: (0, 0))
    outs = (
        jax.ShapeDtypeStruct((frames, 3 * width), jnp.bfloat16),
        jax.ShapeDtypeStruct((frames, 2 * width), jnp.bfloat16),
    )
    return pl.pallas_call(
        functools.partial(attention_kernel, width),
        grid=(HEADS // TOGETHER,),
        in_specs=[whole(qkv), whole(prev), whole(grad)],
        out_specs=[whole(o) for o in outs],
        out_shape=outs,
        cost_estimate=pl.CostEstimate(
            flops=20 * frames * frames * width,
            bytes_accessed=22 * frames * width,
            transcendentals=2 * HEADS * frames * frames,
        ),
    )(qkv, prev, grad)


def bit_of(index, bit):
    return (index // (1 << bit)) % 2


def reduce_kernel(records, scale, *refs):
    frames, before = refs[:records], refs[records : 2 * records]
    own, earlier = refs[2 * records : 3 * records], refs[3 * records : 4 * records]
    returned, w_ref = refs[4 * records : 5 * records - 1], refs[-1]
    out_ref, grad_ref, held, landed, sums, leaving, arriving = refs[5 * records : 5 * records + 7]
    send_sem, recv_sem, back_send_sem, back_recv_sem, load_sem = refs[5 * records + 7 : -1]
    load = pltpu.make_async_copy(refs[5 * records - 1], w_ref, load_sem)
    load.start()
    width = frames[0].shape[1]
    streams, blocks = lax.axis_size("stream"), lax.axis_size("tm")
    stream, block = lax.axis_index("stream"), lax.axis_index("tm")
    stream_bits, block_bits = streams.bit_length() - 1, blocks.bit_length() - 1
    dims = [("stream", b, bit_of(stream, b)) for b in reversed(range(stream_bits))]
    dims += [("tm", b, bit_of(block, b)) for b in reversed(range(block_bits))]
    count = len(dims)
    first = stream_bits - 1
    rest = list(reversed(range(first))) + list(reversed(range(first + 1, count)))
    orders = [[first] + rest[c % len(rest) :] + rest[: c % len(rest)] for c in range(3)]

    def partner(d):
        axis, b, value = dims[d]
        return {axis: (stream if axis == "stream" else block) + (1 - 2 * value) * (1 << b)}

    barrier = pltpu.get_barrier_semaphore()
    for d in range(count):
        pl.semaphore_signal(
            barrier, inc=1, device_id=partner(d), device_id_type=pl.DeviceIdType.MESH
        )
    has_before, has_after = block > 0, block < blocks - 1

    def greet(step):
        pl.semaphore_signal(
            barrier,
            inc=1,
            device_id={"tm": block + step},
            device_id_type=pl.DeviceIdType.MESH,
        )

    pl.when(has_before)(lambda: greet(-1))
    pl.when(has_after)(lambda: greet(1))
    beside = (block + blocks - 1) // blocks + (2 * blocks - 2 - block) // blocks
    pl.semaphore_wait(barrier, count + beside)
    back = pltpu.make_async_remote_copy(
        src_ref=leaving,
        dst_ref=arriving,
        send_sem=back_send_sem,
        recv_sem=back_recv_sem,
        device_id={"tm": block - 1},
        device_id_type=pl.DeviceIdType.MESH,
    )

    def by_columns(store):
        step = 256

        def body(j, carry):
            span = pl.ds(pl.multiple_of(j * step, step), step)
            store(span)
            return carry

        lax.fori_loop(0, width // step, body, 0)

    def returning(span):
        terms = dot(earlier[-1][...], w_ref[span, width:], NT)
        leaving[:, span] = terms.astype(leaving.dtype)

    def own_terms(r, span):
        terms = dot(own[r][...], w_ref[span, :], NT)
        if r < records - 1:
            terms += returned[r][:, span].astype(jnp.float32)
            grad_ref[r, :, span] = terms.astype(grad_ref.dtype)
        else:
            sums[:, span] = terms

    work = [functools.partial(by_columns, functools.partial(own_terms, r)) for r in range(records)]

    rows = width // streams

    def products(parity):
        def body(j, carry):
            piece = 2 * j + parity
            span = pl.ds(pl.multiple_of(piece * rows, rows), rows)
            lead = [bit_of(piece, b) for b in reversed(range(stream_bits))]
            for c in range(3):
                total = 0.0
                for r in range(records):
                    cols = slice(c * width, (c + 1) * width)
                    total += dot(frames[r][:, span], own[r][:, cols], TN)
                    if c > 0:
                        cols = slice((c - 1) * width, c * width)
                        total += dot(before[r][:, span], earlier[r][:, cols], TN)
                shape = held.shape[1 + stream_bits :]
                held[(c, *lead)] = total.astype(held.dtype).reshape(shape)
            return carry

        lax.fori_loop(0, streams // 2, body, 0)

    def region(c, phase, kept):
        index = [slice(None)] * count
        for d in orders[c][:phase]:
            index[d] = dims[d][2]
        last = orders[c][phase]
        index[last] = dims[last][2] if kept else 1 - dims[last][2]
        return (c, *index)

    def copy(c, phase):
        return pltpu.make_async_remote_copy(
            src_ref=held.at[region(c, phase, False)],
            dst_ref=landed.at[region(c, phase, True)],
            send_sem=send_sem.at[c, phase],
            recv_sem=recv_sem.at[c, phase],
            device_id=partner(orders[c][phase]),
            device_id_type=pl.DeviceIdType.MESH,
        )

    def merge(c, phase):
        free = [d for d in range(count) if d not in orders[c][: phase + 1]]

        def body(j, carry):
            kept = list(region(c, phase, True))
            arrived = list(region(c, phase, False))
            for k, d in enumerate(free):
                kept[1 + d] = arrived[1 + d] = bit_of(j, k)
            kept, arrived = tuple(kept), tuple(arrived)
            total = held[kept].astype(jnp.float32) + landed[arrived].astype(jnp.float32)
            if free:
                held[kept] = total.astype(held.dtype)
            else:
                out_ref[:, c * width : (c + 1) * width] = total * scale
            return carry

        if free:
            lax.fori_loop(0, 1 << len(free), body, 0)
        else:
            body(0, 0)

    products(1 - dims[first][2])
    for c in range(3):
        copy(c, 0).start()
    load.wait()
    by_columns(returning)
    pl.when(has_before)(back.start)
    products(dims[first][2])
    for phase in range(count):
        if 0 < phase <= records:
            work[phase - 1]()
        for c in range(3):
            copy(c, phase).wait_recv()
            merge(c, phase)
            if phase + 1 < count:
                copy(c, phase + 1).start()
    for phase in range(count):
        for c in range(3):
            copy(c, phase).wait_send()
    pl.when(has_before)(back.wait_send)
    last = records - 1

    @pl.when(has_after)
    def _():
        back.wait_recv()
        grad_ref[last] = (sums[...] + arriving[...].astype(jnp.float32)).astype(grad_ref.dtype)

    @pl.when(jnp.logical_not(has_after))
    def _():
        grad_ref[last] = sums[...].astype(grad_ref.dtype)


def gradients(frames, before, own, earlier, returned, w_qkv, scale):
    records = len(frames)
    rows, width = frames[0].shape
    devices = lax.axis_size("stream") * lax.axis_size("tm")
    count = devices.bit_length() - 1
    part = pltpu.VMEM((3, *([2] * count), width // devices, width), jnp.bfloat16)
    operands = (*frames, *before, *own, *earlier, *returned, w_qkv)
    return pl.pallas_call(
        functools.partial(reduce_kernel, records, scale),
        in_specs=[pl.BlockSpec(memory_space=pltpu.VMEM)] * (len(operands) - 1)
        + [pl.BlockSpec(memory_space=pl.ANY)],
        out_specs=[pl.BlockSpec(memory_space=pltpu.VMEM)] * 2,
        out_shape=(
            jax.ShapeDtypeStruct((width // devices, 3 * width), jnp.float32),
            jax.ShapeDtypeStruct((records, rows, width), jnp.bfloat16),
        ),
        scratch_shapes=[
            part,
            part,
            pltpu.VMEM((rows, width), jnp.float32),
            pltpu.VMEM((rows, width), jnp.bfloat16),
            pltpu.VMEM((rows, width), jnp.bfloat16),
            pltpu.SemaphoreType.DMA((3, count)),
            pltpu.SemaphoreType.DMA((3, count)),
            pltpu.SemaphoreType.DMA,
            pltpu.SemaphoreType.DMA,
            pltpu.SemaphoreType.DMA,
            pltpu.VMEM(w_qkv.shape, w_qkv.dtype),
        ],
        compiler_params=pltpu.CompilerParams(collective_id=0, has_side_effects=True),
        cost_estimate=pl.CostEstimate(
            flops=20 * records * frames[0].size * width,
            bytes_accessed=22 * records * frames[0].size,
            transcendentals=0,
        ),
    )(*operands)


def local(frames_in, w_qkv, grad_out):
    records, frame_count, width = frames_in.shape
    w_kv = w_qkv[:, width:]
    total_frames = records * frame_count * lax.axis_size("stream") * lax.axis_size("tm")
    before = [passed_along(frames_in[r], "tm", 1) for r in range(records)]
    own, earlier, returned = [], [], []
    joined = [dot(frames_in[r], w_qkv).astype(jnp.bfloat16) for r in range(records)]
    before[0], *joined = lax.optimization_barrier((before[0], *joined))
    for r in range(records):
        prev = dot(before[r], w_kv).astype(jnp.bfloat16)
        d_own, d_earlier = attention(joined[r], prev, grad_out[r])
        if r < records - 1:
            back = dot(d_earlier, w_kv, NT).astype(jnp.bfloat16)
            returned.append(passed_along(back, "tm", -1))
        own.append(d_own)
        earlier.append(d_earlier)
    grad_w, grad_in = gradients(
        [frames_in[r] for r in range(records)],
        before,
        own,
        earlier,
        returned,
        w_qkv,
        float(total_frames) ** (-0.5),
    )
    return (grad_in, grad_w)


def solution(mesh):
    return jax.shard_map(
        local,
        mesh=mesh,
        in_specs=(P("stream", "tm", None), P(), P("stream", "tm", None)),
        out_specs=(P("stream", "tm", None), P(("stream", "tm"), None)),
        check_vma=False,
    )
```
